128 devices in a mesh: dp: 64 (over z, y, x_hi, core), tensor: 2 (over x_lo).
Axes of the slice: x: 4 (x_hi: 2, x_lo: 2; x = x_hi * 2 + x_lo), y: 4, z: 4, core: 2. Of those that a mesh axis runs over, the one named last changes fastest.
Arguments:
- tokens: bfloat16 [65536, 2048], P('dp', 'tensor'), may hold values from -30 to 30
- norm_gain: bfloat16 [2048], P('tensor'), may hold values from 0.5 to 7
- w_query: bfloat16 [2048, 2048], P(None, 'tensor'), may hold values from -0.125 to 0.125
- key_weight: bfloat16 [2048, 1024], P(None, 'tensor'), may hold values from -0.125 to 0.125
- value_weight: bfloat16 [2048, 1024], P(None, 'tensor'), may hold values from -0.125 to 0.125
- w_out: bfloat16 [2048, 2048], P('tensor'), may hold values from -0.125 to 0.125
- valid_lengths: int32 [64], P('dp'), may hold values from 1 to 1024, as said below
- earlier_cache_pages: bfloat16 [4096, 2, 8, 32, 128], P('dp', None, 'tensor'), may hold values from -6 to 6
- page_owner: int32 [4096], P('dp'), may hold values from 0 to 63, as said below
- page_slot: int32 [4096], P('dp'), may hold values from 0 to 63, as said below
- page_live: int32 [4096], P('dp'), may hold values 0 or 1
Outputs:
- mixed: bfloat16 [65536, 2048], P('dp', 'tensor')
- decode_pages: bfloat16 [8, 4096, 2, 32, 128], P('tensor', 'dp')
The draws below stay inside these ranges and needn't reach their ends.
Inputs may be any that keep to these rules, and one draw needn't show every extreme that they name: `valid_lengths`: some request has all 1024 tokens valid. `page_owner`: the 64 pages of each source dp index name every dp index exactly once. `page_slot`: pages that name the same owner carry different slots.
All inputs are finite; a program needn't handle non-finite values. No bound on the sum of `page_live` on one device may be relied on, other than what follows from the above.
Results may differ from the reference program's by a relative error of at most 0.01065.
The reference program's roundings to bfloat16 on the way count: a program that leaves them out, or rounds other values in their place, can miss the bound.
Values may be sent and summed in bfloat16 or wider, within the bound.
A program may use at most 192 MiB of HBM per device.

```python
import math
import jax
import jax.numpy as jnp
from jax import lax

MODEL_WIDTH = 2048
QUERY_HEADS = 16
KEY_VALUE_HEADS = 8
HEAD_SIZE = 128
REQUEST_TOKENS = 1024
PAGE_TOKENS = 32
TOKENS = 65536
PAGES_PER_RANK = 64
PAGE_SLOTS = 4096
N_DP = 64
N_TENSOR = 2


def page_layout(key):
    base_key = jax.random.fold_in(key, 11)
    owner_key, slot_key = jax.random.split(base_key)

    def one_order(sub_key):
        return jax.random.permutation(sub_key, N_DP).astype(jnp.int32)
    owner = jax.vmap(one_order)(jax.random.split(owner_key, N_DP))
    slot_orders = jax.vmap(one_order)(jax.random.split(slot_key, N_DP))
    source_rows = jnp.broadcast_to(jnp.arange(N_DP)[:, None], (N_DP, N_DP))
    slot = slot_orders[owner, source_rows]
    return (owner.reshape(-1).astype(jnp.int32), slot.reshape(-1).astype(jnp.int32))


def draw_page_owner(key, part):
    return page_layout(key)[0]


def draw_page_slot(key, part):
    return page_layout(key)[1]


def draw_valid_lengths(key, part):
    first_key, second_key = jax.random.split(key)
    raw = jax.random.randint(first_key, (N_DP,), 0, REQUEST_TOKENS)
    lengths = 1 + raw * raw // REQUEST_TOKENS
    chosen = jax.random.randint(second_key, (), 0, N_DP)
    return jnp.where(jnp.arange(N_DP) == chosen, REQUEST_TOKENS, lengths).astype(jnp.int32)


def draw_tokens(key, part):
    first_key, second_key = jax.random.split(key)
    row_scale = jnp.exp(jax.random.uniform(second_key, (TOKENS, 1), jnp.float32, math.log(0.3), math.log(3.0)))
    ramp = jnp.arange(MODEL_WIDTH, dtype=jnp.float32) / (MODEL_WIDTH - 1)
    base = jax.random.truncated_normal(first_key, -6.0, 6.0, (TOKENS, MODEL_WIDTH), jnp.float32)
    col_scale = 0.5 + ramp
    return (base * row_scale * col_scale[None, :]).astype(jnp.bfloat16)


def draw_norm_gain(key, part):
    return jnp.exp(jax.random.uniform(key, (MODEL_WIDTH,), jnp.float32, math.log(0.5), math.log(1.5))).astype(jnp.bfloat16)


def plant(drawn, rng, least, largest):
    longest = drawn.shape.index(max(drawn.shape))
    spots = []
    for shift in (0, 1):
        where = [jax.random.randint(jax.random.fold_in(rng, axis), (), 0, length) for axis, length in enumerate(drawn.shape)]
        where[longest] = (where[longest] + shift) % drawn.shape[longest]
        spots.append(tuple(where))
    return drawn.at[spots[0]].set(least).at[spots[1]].set(largest)


def block_scale(key, dims, shards, low, top_value):
    def one(position, blocks):
        heights = jax.random.uniform(jax.random.fold_in(jax.random.fold_in(key, 6), position), (blocks,), jnp.float32, low / len(shards), top_value / len(shards))
        return jnp.repeat(jnp.exp(heights), dims[position] // blocks).reshape((-1,) + (1,) * (len(dims) - position - 1))

    factor_of = one(*shards[0])
    for cut in shards[1:]:
        factor_of = factor_of * one(*cut)
    return factor_of


def normal_values(own_key, dims, scale, bound, shards=(), kind=jnp.bfloat16):
    factor_of = block_scale(own_key, dims, shards, -0.22, 0.18) if shards else 1.0
    values = jax.random.normal(own_key, dims, jnp.float32) * scale * factor_of
    return jnp.minimum(jnp.maximum(values, -bound), bound).astype(kind)


def setup_inputs(seed: int = 0) -> dict:
    seeds = jax.random.split(jax.random.key(seed), 12)
    tokens = draw_tokens(jax.random.fold_in(seeds[11], 71), 0)
    norm_gain = draw_norm_gain(jax.random.fold_in(seeds[11], 71), 0)
    w_query = normal_values(seeds[2], (MODEL_WIDTH, QUERY_HEADS * HEAD_SIZE), MODEL_WIDTH ** -0.5, 0.125, ((1, 2),))
    key_weight = normal_values(seeds[3], (MODEL_WIDTH, KEY_VALUE_HEADS * HEAD_SIZE), MODEL_WIDTH ** -0.5, 0.125, ((1, 2),))
    value_weight = normal_values(seeds[4], (MODEL_WIDTH, KEY_VALUE_HEADS * HEAD_SIZE), MODEL_WIDTH ** -0.5, 0.125, ((1, 2),))
    w_out = normal_values(seeds[5], (QUERY_HEADS * HEAD_SIZE, MODEL_WIDTH), (QUERY_HEADS * HEAD_SIZE) ** -0.5, 0.125, ((0, 2),))
    valid_lengths = draw_valid_lengths(jax.random.fold_in(seeds[11], 71), 0)
    earlier_cache_pages = normal_values(seeds[7], (PAGE_SLOTS, 2, KEY_VALUE_HEADS, PAGE_TOKENS, HEAD_SIZE), 1.0, 6.0, ((0, 64), (2, 2)))
    page_owner = draw_page_owner(jax.random.fold_in(seeds[11], 71), 0)
    page_slot = draw_page_slot(jax.random.fold_in(seeds[11], 71), 0)
    page_live = plant((jax.random.randint(seeds[10], (PAGE_SLOTS,), 0, 8) < 7).astype(jnp.int32), jax.random.fold_in(seeds[10], 1), 0, 1)
    return dict(tokens=tokens, norm_gain=norm_gain, w_query=w_query, key_weight=key_weight, value_weight=value_weight, w_out=w_out, valid_lengths=valid_lengths, earlier_cache_pages=earlier_cache_pages, page_owner=page_owner, page_slot=page_slot, page_live=page_live)


NORM_EPS = 1e-05
ROPE_THETA = 1000000.0

def rotary_tables(values, token_positions):
    dim = values.shape[-1]
    half = dim // 2
    freqs = ROPE_THETA ** (-jnp.arange(half, dtype=jnp.float32) * 2.0 / dim)
    angles = token_positions.astype(jnp.float32)[:, None] * freqs[None, :]
    cosine = jnp.cos(angles)[:, None, :]
    sine = jnp.sin(angles)[:, None, :]
    first = values[..., :half]
    second = values[..., half:]
    return jnp.concatenate([first * cosine - second * sine, second * cosine + first * sine], axis=-1)

def normalize(values, gain):
    mean_sq = lax.optimization_barrier(jnp.mean(values * values, axis=-1, keepdims=True))
    return (values * lax.rsqrt(mean_sq + NORM_EPS) * gain.astype(jnp.float32)).astype(jnp.bfloat16)

def reference(tokens, norm_gain, w_query, key_weight, value_weight, w_out, valid_lengths, earlier_cache_pages, page_owner, page_slot, page_live):
    out_groups = w_out.astype(jnp.float32).reshape(N_TENSOR, QUERY_HEADS * HEAD_SIZE // N_TENSOR, MODEL_WIDTH)
    token_positions = jnp.arange(REQUEST_TOKENS)

    def prefill_request(inputs):
        request_rows, length = inputs
        values = request_rows.astype(jnp.float32)
        normed = normalize(values, norm_gain)
        query_raw = jnp.dot(normed, w_query, preferred_element_type=jnp.float32)
        key_unrotated = jnp.dot(normed, key_weight, preferred_element_type=jnp.float32)
        value_projected = jnp.dot(normed, value_weight, preferred_element_type=jnp.float32)
        query_vectors = rotary_tables(query_raw.reshape(REQUEST_TOKENS, QUERY_HEADS, HEAD_SIZE), token_positions).astype(jnp.bfloat16)
        query_vectors = query_vectors.reshape(REQUEST_TOKENS, KEY_VALUE_HEADS, QUERY_HEADS // KEY_VALUE_HEADS, HEAD_SIZE)
        key_turned = rotary_tables(key_unrotated.reshape(REQUEST_TOKENS, KEY_VALUE_HEADS, HEAD_SIZE), token_positions).astype(jnp.bfloat16)
        value_halfprec = value_projected.reshape(REQUEST_TOKENS, KEY_VALUE_HEADS, HEAD_SIZE).astype(jnp.bfloat16)
        scores = jnp.einsum('qgrd,kgd->grqk', query_vectors.astype(jnp.float32), key_turned.astype(jnp.float32)) * HEAD_SIZE ** (-0.5)
        query_pos = jnp.arange(REQUEST_TOKENS)[:, None]
        key_pos = jnp.arange(REQUEST_TOKENS)[None, :]
        allowed = (key_pos <= query_pos) & (key_pos < length)
        scores = jnp.where(allowed, scores, -1e+30)
        row_peak = lax.optimization_barrier(jnp.max(scores, axis=-1, keepdims=True))
        exponent = jnp.exp(scores - row_peak)
        attn_weights = (exponent / lax.optimization_barrier(jnp.sum(exponent, axis=-1, keepdims=True))).astype(jnp.bfloat16)
        attended = jnp.einsum('grqk,kgd->qgrd', attn_weights.astype(jnp.float32), value_halfprec.astype(jnp.float32))
        attended = attended.astype(jnp.bfloat16).reshape(REQUEST_TOKENS, QUERY_HEADS * HEAD_SIZE)
        grouped = attended.astype(jnp.float32).reshape(REQUEST_TOKENS, N_TENSOR, QUERY_HEADS * HEAD_SIZE // N_TENSOR)
        partial_value = jnp.einsum('tgc,gcd->gtd', grouped, out_groups).astype(jnp.bfloat16)
        summed = lax.optimization_barrier(jnp.sum(partial_value.astype(jnp.float32), axis=0))
        return (values + summed).astype(jnp.bfloat16)
    mixed = lax.map(prefill_request, (tokens.reshape(N_DP, REQUEST_TOKENS, MODEL_WIDTH), valid_lengths))
    mixed = mixed.reshape(TOKENS, MODEL_WIDTH)
    target = jnp.where(page_live == 1, page_slot, PAGES_PER_RANK).astype(jnp.int32)
    owner_placed = jnp.zeros((N_DP, PAGES_PER_RANK, 2, KEY_VALUE_HEADS, PAGE_TOKENS, HEAD_SIZE), jnp.bfloat16)
    owner_placed = owner_placed.at[page_owner, target].set(earlier_cache_pages, mode='drop')
    owner_placed = owner_placed.reshape(PAGE_SLOTS, 2, KEY_VALUE_HEADS, PAGE_TOKENS, HEAD_SIZE)
    decode_pages = jnp.transpose(owner_placed, (2, 0, 1, 3, 4))
    return (mixed, decode_pages)
```

```python
import jax
import jax.numpy as jnp
from jax import lax
from jax.sharding import PartitionSpec as P

MODEL_WIDTH = 2048
HEAD_SIZE = 128


NORM_EPS = 1e-05
ROPE_THETA = 1000000.0


def rotary_tables(values, token_positions):
    dim = values.shape[-1]
    half = dim // 2
    freqs = ROPE_THETA ** (-jnp.arange(half, dtype=jnp.float32) * 2.0 / dim)
    angles = token_positions.astype(jnp.float32)[:, None] * freqs[None, :]
    cosine = jnp.cos(angles)[:, None, :]
    sine = jnp.sin(angles)[:, None, :]
    first = values[..., :half]
    second = values[..., half:]
    return jnp.concatenate(
        [first * cosine - second * sine, second * cosine + first * sine], axis=-1
    )


def project_inputs(tokens, norm_gain, w_query, key_weight, value_weight):
    full_rows = lax.all_gather(tokens, "tensor", axis=1, tiled=True)
    full_gain = lax.all_gather(norm_gain, "tensor", axis=0, tiled=True)
    values = full_rows.astype(jnp.float32)
    mean_sq = jnp.mean(values * values, axis=-1, keepdims=True)
    normed = (values * lax.rsqrt(mean_sq + NORM_EPS) * full_gain.astype(jnp.float32)).astype(
        jnp.bfloat16
    )
    return (
        jnp.dot(normed, w_query, preferred_element_type=jnp.float32),
        jnp.dot(normed, key_weight, preferred_element_type=jnp.float32),
        jnp.dot(normed, value_weight, preferred_element_type=jnp.float32),
    )


def prefill_layer(tokens, norm_gain, w_query, key_weight, value_weight, w_out, valid_lengths):
    query_raw, key_unrotated, value_projected = project_inputs(
        tokens, norm_gain, w_query, key_weight, value_weight
    )
    token_count = tokens.shape[0]
    heads_query = w_query.shape[1] // HEAD_SIZE
    heads_kv = key_weight.shape[1] // HEAD_SIZE
    token_positions = jnp.arange(token_count)
    query_vectors = rotary_tables(
        query_raw.reshape(token_count, heads_query, HEAD_SIZE), token_positions
    ).astype(jnp.bfloat16)
    query_vectors = query_vectors.reshape(token_count, heads_kv, heads_query // heads_kv, HEAD_SIZE)
    key_turned = rotary_tables(
        key_unrotated.reshape(token_count, heads_kv, HEAD_SIZE), token_positions
    ).astype(jnp.bfloat16)
    value_halfprec = value_projected.reshape(token_count, heads_kv, HEAD_SIZE).astype(jnp.bfloat16)
    length = valid_lengths[0]
    block_rows = min(512, token_count)
    outputs = []
    for block_index in range(token_count // block_rows):
        first_row = block_index * block_rows
        query_block = query_vectors[first_row : first_row + block_rows]
        scores = jnp.einsum(
            "qgrd,kgd->grqk", query_block, key_turned, preferred_element_type=jnp.float32
        ) * HEAD_SIZE ** (-0.5)
        query_pos = first_row + jnp.arange(block_rows)
        key_pos = jnp.arange(token_count)
        allowed = (key_pos[None, :] <= query_pos[:, None]) & (key_pos[None, :] < length)
        scores = jnp.where(allowed, scores, -1e30)
        row_peak = jnp.max(scores, axis=-1, keepdims=True)
        exponent = jnp.exp(scores - row_peak)
        attn_weights = (exponent / jnp.sum(exponent, axis=-1, keepdims=True)).astype(jnp.bfloat16)
        block_out = jnp.einsum(
            "grqk,kgd->qgrd", attn_weights, value_halfprec, preferred_element_type=jnp.float32
        )
        outputs.append(block_out.astype(jnp.bfloat16).reshape(block_rows, heads_query * HEAD_SIZE))
    attended = jnp.concatenate(outputs, axis=0)
    summed = lax.psum_scatter(
        lax.dot_general(
            w_out, attended, (((0,), (1,)), ((), ())), preferred_element_type=jnp.float32
        ).astype(jnp.bfloat16),
        "tensor",
        scatter_dimension=0,
        tiled=True,
    ).astype(jnp.float32)
    return (tokens.astype(jnp.float32) + summed.T).astype(jnp.bfloat16)


def move_pages(earlier_cache_pages, page_owner, page_slot, page_live):
    peer_count = lax.axis_size("dp")
    slot_count = earlier_cache_pages.shape[0]
    order = jnp.arange(slot_count, dtype=jnp.int32)
    page_for_owner = jnp.zeros((peer_count,), jnp.int32).at[page_owner].set(order)
    outgoing = jnp.take(earlier_cache_pages, page_for_owner, axis=0)
    labels = jnp.where(page_live == 1, page_slot, -1)
    slot_tags = jnp.take(labels, page_for_owner, axis=0)
    incoming = lax.all_to_all(outgoing, "dp", split_axis=0, concat_axis=0, tiled=True)
    in_tags = lax.all_to_all(slot_tags, "dp", split_axis=0, concat_axis=0, tiled=True)
    target = jnp.where(in_tags >= 0, in_tags, slot_count).astype(jnp.int32)
    source_of = (
        jnp.full((slot_count + 1,), peer_count, jnp.int32).at[target].set(
            jnp.arange(peer_count, dtype=jnp.int32)
        )[:slot_count]
    )
    filled = source_of < peer_count
    heads_first = jnp.transpose(incoming, (2, 0, 1, 3, 4))
    placed = jnp.take(heads_first, jnp.minimum(source_of, peer_count - 1), axis=1)
    return jnp.where(filled[None, :, None, None, None], placed, jnp.zeros_like(placed))


def on_device(
    tokens,
    norm_gain,
    w_query,
    key_weight,
    value_weight,
    w_out,
    valid_lengths,
    earlier_cache_pages,
    page_owner,
    page_slot,
    page_live,
):
    mixed = prefill_layer(
        tokens, norm_gain, w_query, key_weight, value_weight, w_out, valid_lengths
    )
    decode_pages = move_pages(earlier_cache_pages, page_owner, page_slot, page_live)
    return (mixed, decode_pages)


def solution(mesh):
    return jax.shard_map(
        on_device,
        mesh=mesh,
        in_specs=(
            P("dp", "tensor"),
            P("tensor"),
            P(None, "tensor"),
            P(None, "tensor"),
            P(None, "tensor"),
            P("tensor", None),
            P("dp"),
            P("dp", None, "tensor", None, None),
            P("dp"),
            P("dp"),
            P("dp"),
        ),
        out_specs=(P("dp", "tensor"), P("tensor", "dp", None, None, None)),
        check_vma=False,
    )
```

```python
import jax
import jax.numpy as jnp
from jax import lax
from jax.sharding import PartitionSpec as P
from jax.experimental import pallas as pl
from jax.experimental.pallas import tpu as pltpu
import functools

MODEL_WIDTH = 2048
HEAD_SIZE = 128


NORM_EPS = 1e-05
ROPE_THETA = 1000000.0


def rotary_tables(values, token_positions):
    dim = values.shape[-1]
    half = dim // 2
    freqs = ROPE_THETA ** (-jnp.arange(half, dtype=jnp.float32) * 2.0 / dim)
    angles = token_positions.astype(jnp.float32)[:, None] * freqs[None, :]
    cosine = jnp.cos(angles)[:, None, :]
    sine = jnp.sin(angles)[:, None, :]
    first = values[..., :half]
    second = values[..., half:]
    return jnp.concatenate(
        [first * cosine - second * sine, second * cosine + first * sine], axis=-1
    )


def project_inputs(tokens, norm_gain, w_query, key_weight, value_weight, held):
    half_width = tokens.shape[1]
    my_offset = lax.axis_index("tensor") * half_width
    other_offset = (1 - lax.axis_index("tensor")) * half_width
    swap = [(0, 1), (1, 0)]
    other_rows = lax.ppermute(tokens, "tensor", perm=swap)
    other_gain = lax.ppermute(norm_gain, "tensor", perm=swap)
    full_rows = jnp.zeros((tokens.shape[0], 2 * half_width), tokens.dtype)
    full_rows = lax.dynamic_update_slice_in_dim(full_rows, tokens, my_offset, axis=1)
    full_rows = lax.dynamic_update_slice_in_dim(full_rows, other_rows, other_offset, axis=1)
    full_gain = jnp.zeros((2 * half_width,), norm_gain.dtype)
    full_gain = lax.dynamic_update_slice_in_dim(full_gain, norm_gain, my_offset, axis=0)
    full_gain = lax.dynamic_update_slice_in_dim(full_gain, other_gain, other_offset, axis=0)
    values = full_rows.astype(jnp.float32)
    mean_sq = jnp.mean(values * values, axis=-1, keepdims=True)
    normed = (values * lax.rsqrt(mean_sq + NORM_EPS) * full_gain.astype(jnp.float32)).astype(
        jnp.bfloat16
    )
    projected = (
        jnp.dot(normed, w_query, preferred_element_type=jnp.float32),
        jnp.dot(normed, key_weight, preferred_element_type=jnp.float32),
        jnp.dot(normed, value_weight, preferred_element_type=jnp.float32),
    )
    return lax.optimization_barrier((projected, held))


def prefill_layer(tokens, norm_gain, w_query, key_weight, value_weight, w_out, valid_lengths, held, stage_two):
    (query_raw, key_unrotated, value_projected), held = project_inputs(
        tokens, norm_gain, w_query, key_weight, value_weight, held
    )
    moved = stage_two(held)
    token_count = tokens.shape[0]
    heads_query = w_query.shape[1] // HEAD_SIZE
    heads_kv = key_weight.shape[1] // HEAD_SIZE
    token_positions = jnp.arange(token_count)
    query_vectors = rotary_tables(
        query_raw.reshape(token_count, heads_query, HEAD_SIZE), token_positions
    ).astype(jnp.bfloat16)
    query_vectors = query_vectors.reshape(token_count, heads_kv, heads_query // heads_kv, HEAD_SIZE)
    key_turned = rotary_tables(
        key_unrotated.reshape(token_count, heads_kv, HEAD_SIZE), token_positions
    ).astype(jnp.bfloat16)
    value_halfprec = value_projected.reshape(token_count, heads_kv, HEAD_SIZE).astype(jnp.bfloat16)
    length = valid_lengths[0]
    block_rows = min(512, token_count)
    half_width = w_out.shape[1] // 2
    my_rows = lax.axis_index("tensor") * half_width
    other_rows = (1 - lax.axis_index("tensor")) * half_width
    outputs = []
    for block_index in range(token_count // block_rows):
        first_row = block_index * block_rows
        query_block = query_vectors[first_row : first_row + block_rows]
        key_count = first_row + block_rows
        scores = jnp.einsum(
            "qgrd,kgd->grqk", query_block, key_turned[:key_count],
            preferred_element_type=jnp.float32,
        ) * HEAD_SIZE ** (-0.5)
        query_pos = first_row + jnp.arange(block_rows)
        key_pos = jnp.arange(key_count)
        allowed = (key_pos[None, :] <= query_pos[:, None]) & (key_pos[None, :] < length)
        scores = jnp.where(allowed, scores, -1e30)
        row_peak = jnp.max(scores, axis=-1, keepdims=True)
        exponent = jnp.exp(scores - row_peak)
        attn_weights = (exponent / jnp.sum(exponent, axis=-1, keepdims=True)).astype(jnp.bfloat16)
        block_out = jnp.einsum(
            "grqk,kgd->qgrd", attn_weights, value_halfprec[:key_count],
            preferred_element_type=jnp.float32,
        )
        block_attended = block_out.astype(jnp.bfloat16).reshape(block_rows, heads_query * HEAD_SIZE)
        partial_value = lax.dot_general(
            w_out, block_attended, (((0,), (1,)), ((), ())),
            preferred_element_type=jnp.float32,
        ).astype(jnp.bfloat16)
        own_part = lax.dynamic_slice_in_dim(partial_value, my_rows, half_width, axis=0)
        sent_part = lax.dynamic_slice_in_dim(partial_value, other_rows, half_width, axis=0)
        got_part = lax.ppermute(sent_part, "tensor", perm=[(0, 1), (1, 0)])
        outputs.append(own_part.astype(jnp.float32) + got_part.astype(jnp.float32))
    summed = jnp.concatenate(outputs, axis=1)
    return (tokens.astype(jnp.float32) + summed.T).astype(jnp.bfloat16), moved


def place_kernel(source_ref, keep_ref, recv_ref, out_ref):
    slots = out_ref.shape[1]
    pairs = recv_ref.shape[1]
    heads = recv_ref.shape[2]

    def body(slot, carry):
        source = source_ref[slot]
        keep = keep_ref[slot] > 0
        for pair in range(pairs):
            for head in range(heads):
                block = recv_ref[source, pair, head]
                out_ref[head, slot, pair] = jnp.where(keep, block, jnp.zeros_like(block))
        return carry

    lax.fori_loop(0, slots, body, 0)


def place(incoming, source_of, keep):
    count, pairs, heads, rows, lanes = incoming.shape
    return pl.pallas_call(
        place_kernel,
        out_shape=jax.ShapeDtypeStruct((heads, count, pairs, rows, lanes), incoming.dtype),
        in_specs=[
            pl.BlockSpec(memory_space=pltpu.SMEM),
            pl.BlockSpec(memory_space=pltpu.SMEM),
            pl.BlockSpec(memory_space=pltpu.VMEM),
        ],
        out_specs=pl.BlockSpec(memory_space=pltpu.VMEM),
        cost_estimate=pl.CostEstimate(
            flops=0, bytes_accessed=2 * incoming.size * incoming.dtype.itemsize, transcendentals=0
        ),
    )(source_of, keep, incoming)


def move_pages(earlier_cache_pages, page_owner, page_slot, page_live):
    peer_count = lax.axis_size("dp")
    slot_count = earlier_cache_pages.shape[0]
    inner = 4
    outer = peer_count // inner
    me = lax.axis_index("dp")
    me_in = me % inner
    me_out = me // inner
    order = jnp.arange(slot_count, dtype=jnp.int32)
    page_for_owner = jnp.zeros((peer_count,), jnp.int32).at[page_owner].set(order)
    outgoing = jnp.take(earlier_cache_pages, page_for_owner, axis=0, mode="clip")
    labels = jnp.where(page_live == 1, page_slot, -1)
    slot_tags = jnp.take(labels, page_for_owner, axis=0, mode="clip")
    page_shape = outgoing.shape[1:]
    by_owner = outgoing.reshape((outer, inner) + page_shape)
    first = [lax.dynamic_index_in_dim(by_owner, me_in, axis=1, keepdims=False)]
    for shift in range(1, inner):
        target_in = (me_in + shift) % inner
        sent = lax.dynamic_index_in_dim(by_owner, target_in, axis=1, keepdims=False)
        pairs = [(d, (d // inner) * inner + (d % inner + shift) % inner) for d in range(peer_count)]
        first.append(lax.ppermute(sent, "dp", perm=pairs))
    first = jnp.stack(first, axis=0)
    return first, outgoing.shape, slot_tags


def move_pages_second(first, page_shape):
    peer_count = first.shape[0] * first.shape[1]
    inner = first.shape[0]
    outer = first.shape[1]
    me = lax.axis_index("dp")
    me_in = me % inner
    me_out = me // inner
    second = [lax.dynamic_index_in_dim(first, me_out, axis=1, keepdims=False)]
    for shift in range(1, outer):
        target_out = (me_out + shift) % outer
        sent = lax.dynamic_index_in_dim(first, target_out, axis=1, keepdims=False)
        pairs = [(d, ((d // inner + shift) % outer) * inner + d % inner) for d in range(peer_count)]
        second.append(lax.ppermute(sent, "dp", perm=pairs))
    incoming = jnp.stack(second, axis=0).reshape((peer_count,) + page_shape[1:])
    return incoming


def tags_at_positions(slot_tags):
    peer_count = slot_tags.shape[0]
    inner = 4
    outer = peer_count // inner
    me = lax.axis_index("dp")
    me_in = me % inner
    me_out = me // inner
    tag_table = lax.all_gather(slot_tags, "dp", axis=0, tiled=False)
    position = jnp.arange(peer_count, dtype=jnp.int32)
    source = ((me_out - position // inner) % outer) * inner + (me_in - position % inner) % inner
    my_column = lax.dynamic_index_in_dim(tag_table, me, axis=1, keepdims=False)
    return jnp.take(my_column, source, axis=0, mode="clip")


def place_pages(incoming, in_tags):
    peer_count = incoming.shape[0]
    slot_count = incoming.shape[0]
    target = jnp.where(in_tags >= 0, in_tags, slot_count).astype(jnp.int32)
    source_of = (
        jnp.full((slot_count + 1,), peer_count, jnp.int32).at[target].set(
            jnp.arange(peer_count, dtype=jnp.int32)
        )[:slot_count]
    )
    keep = (source_of < peer_count).astype(jnp.int32)
    return place(incoming, jnp.minimum(source_of, peer_count - 1), keep)


def on_device(
    tokens,
    norm_gain,
    w_query,
    key_weight,
    value_weight,
    w_out,
    valid_lengths,
    earlier_cache_pages,
    page_owner,
    page_slot,
    page_live,
):
    first, page_shape, slot_tags = move_pages(
        earlier_cache_pages, page_owner, page_slot, page_live
    )
    mixed, incoming = prefill_layer(
        tokens, norm_gain, w_query, key_weight, value_weight, w_out, valid_lengths,
        first, lambda held: move_pages_second(held, page_shape),
    )
    decode_pages = place_pages(incoming, tags_at_positions(slot_tags))
    return (mixed, decode_pages)


def solution(mesh):
    return jax.shard_map(
        on_device,
        mesh=mesh,
        in_specs=(
            P("dp", "tensor"),
            P("tensor"),
            P(None, "tensor"),
            P(None, "tensor"),
            P(None, "tensor"),
            P("tensor", None),
            P("dp"),
            P("dp", None, "tensor", None, None),
            P("dp"),
            P("dp"),
            P("dp"),
        ),
        out_specs=(P("dp", "tensor"), P("tensor", "dp", None, None, None)),
        check_vma=False,
    )
```
